768 devices in a mesh: row: 12 (over z), col: 64 (over x, y, core).
Axes of the slice: x: 4, y: 8, z: 12, core: 2. Of those that a mesh axis runs over, the one named last changes fastest.
Arguments:
- user_factors: bfloat16 [24576, 128], P(('row', 'col')), may hold values from -1.796875 to 1.796875
- item_factors: bfloat16 [64, 768, 128], P('col', 'row'), may hold values from -1.796875 to 1.796875
- ratings: bfloat16 [12, 64, 36, 128, 128], P('row', 'col'), may hold values from 0 to 8, as said below
- tile_cell: int32 [12, 64, 36], P('row', 'col'), may hold values from 0 to 95, as said below
- keep_count: int32 [12, 64], P('row', 'col'), may hold values from 1 to 24, as said below
- send_count: int32 [12, 64, 12], P('row', 'col'), may hold values from 0 to 2, as said below
- user_nbrs: int32 [24576, 16], P(('row', 'col')), may hold values from 0 to 2047
- item_nbrs: int32 [64, 768, 16], P('col', 'row'), may hold values from 0 to 767
Outputs:
- grad_users: float32 [24576, 128], P(('row', 'col'))
- grad_items: float32 [64, 768, 128], P('col', 'row')
The draws below stay inside these ranges and needn't reach their ends.
Inputs may be any that keep to these rules, and one draw needn't show every extreme that they name: `ratings`: zero marks an unobserved entry; a nonzero value is at least 0.25. `tile_cell`: cells are distinct within a device; cell a * 6 + b is user subtile a of the device's user block and item subtile b of its item block. keep_count plus the sum of send_count is at most 36 on every device and equals 36 on some device of every item block. `send_count`: A device assigns no slots to itself and at most 2 to each other device of its item block; the assigned slots follow its kept slots in the order of the receiving devices; some device assigns exactly 2 to some peer. `user_nbrs`: neighbours index rows of the user's own block. `item_nbrs`: neighbours index rows of the item's own block.
All inputs are finite; a program needn't handle non-finite values.
Results may differ from the reference program's by a relative error of at most 0.0012.
Values may be sent and summed in bfloat16 or wider, within the bound.
A program may use at most 32 MiB of HBM per device.

```python
import jax
import jax.numpy as jnp
from jax import lax

RANK = 128
TILE = 128
UT = 16
VT = 6
SLOTS = 36
PEER = 2
KNN = 16
UBLK = 2048
USERS = 24576
VBLK = 768
N_ROW = 12
N_COL = 64


def tile_plan(key):
    base_key = jax.random.fold_in(key, 7301)
    heavy = jax.random.randint(jax.random.fold_in(base_key, 1), (N_COL,), 0, N_ROW)
    marked = jax.random.randint(jax.random.fold_in(base_key, 5), (), 0, N_COL)
    light = jax.random.randint(jax.random.fold_in(base_key, 2), (N_ROW, N_COL), SLOTS // 6, SLOTS // 3 + 1)
    rows = jnp.arange(N_ROW)[:, None]
    columns = jnp.arange(N_COL)[None, :]
    is_marked_col = columns == marked
    next_row = (heavy[None, :] + 1) % N_ROW
    light = jnp.where(is_marked_col & (rows == next_row), SLOTS // 3, light)
    is_heavy = rows == heavy[None, :]
    counts = jnp.where(is_heavy, SLOTS, light)
    peer_draw = jax.random.randint(jax.random.fold_in(base_key, 3), (N_ROW, N_COL, N_ROW), 1, PEER + 1)
    peer_draw = jnp.where(is_marked_col[:, :, None], 1, peer_draw)
    peers = jnp.arange(N_ROW)[None, None, :]
    owner = jnp.arange(N_ROW)[:, None, None]
    first = (owner + 1) % N_ROW
    per_peer = jnp.where(peers == first, PEER, peer_draw)
    per_peer = jnp.where(peers == owner, 0, per_peer)
    sends = jnp.where(is_heavy[:, :, None], per_peer, 0)
    keep = counts - jnp.sum(sends, axis=2)
    scores = jax.random.randint(jax.random.fold_in(base_key, 4), (N_ROW, N_COL, UT * VT), 0, 2 ** 20)
    scores = scores * (UT * VT) + jnp.arange(UT * VT)[None, None, :]
    order = jnp.argsort(scores, axis=2)
    cells = order[:, :, :SLOTS]
    return (cells.astype(jnp.int32), keep.astype(jnp.int32), sends.astype(jnp.int32))


def draw_tile_cell(key, part):
    return tile_plan(key)[0]


def draw_keep_count(key, part):
    return tile_plan(key)[1]


def draw_send_count(key, part):
    return tile_plan(key)[2]


def draw_ratings(key, part):
    shape = (N_ROW, N_COL, SLOTS, TILE, TILE)
    seen = jax.random.uniform(jax.random.fold_in(key, 11), shape) < 0.4
    level = jnp.exp(jax.random.uniform(jax.random.fold_in(key, 12), shape, minval=jnp.log(0.25), maxval=jnp.log(8.0)))
    return jnp.where(seen, level, 0.0).astype(jnp.float32).astype(jnp.bfloat16)


def place_ends(values, own_key, low, largest):
    index_at = [jax.random.randint(jax.random.fold_in(own_key, axis), (), 0, length) for axis, length in enumerate(values.shape)]
    longest = values.shape.index(max(values.shape))
    neighbour = index_at[:longest] + [(index_at[longest] + 1) % values.shape[longest]] + index_at[longest + 1:]
    return values.at[tuple(index_at)].set(low).at[tuple(neighbour)].set(largest)


def shard_levels(rng, shape, pieces, smallest, top_value):
    loudness, own = 1.0, jax.random.fold_in(rng, 6)
    for position, shards_of in pieces:
        heights = jnp.exp(jax.random.uniform(jax.random.fold_in(own, position), (shards_of,), jnp.float32, smallest / len(pieces), top_value / len(pieces)))
        loudness = loudness * jnp.repeat(heights, shape[position] // shards_of).reshape([-1 if axis == position else 1 for axis in range(len(shape))])
    return loudness


def bell_draw(key, dims, deviation, limit, cuts=(), held_as=jnp.bfloat16):
    factor_of = shard_levels(key, dims, cuts, -0.22, 0.18) if cuts else 1.0
    array = jax.random.normal(key, dims, jnp.float32) * deviation * factor_of
    return jnp.minimum(jnp.maximum(array, -limit), limit).astype(held_as)


def setup_inputs(seed: int = 0) -> dict:
    seeds = jax.random.split(jax.random.key(seed), 9)
    return {
        "user_factors": bell_draw(seeds[0], (USERS, RANK), 0.3, 1.796875, ((0, 768),)),
        "item_factors": bell_draw(seeds[1], (N_COL, VBLK, RANK), 0.3, 1.796875, ((0, 64), (1, 12))),
        "ratings": draw_ratings(jax.random.fold_in(seeds[8], 71), 0),
        "tile_cell": draw_tile_cell(jax.random.fold_in(seeds[8], 71), 0),
        "keep_count": draw_keep_count(jax.random.fold_in(seeds[8], 71), 0),
        "send_count": draw_send_count(jax.random.fold_in(seeds[8], 71), 0),
        "user_nbrs": place_ends(jax.random.randint(seeds[6], (USERS, KNN), 0, UBLK), jax.random.fold_in(seeds[6], 1), 0, UBLK - 1).astype(jnp.int32),
        "item_nbrs": place_ends(jax.random.randint(seeds[7], (N_COL, VBLK, KNN), 0, VBLK), jax.random.fold_in(seeds[7], 1), 0, VBLK - 1).astype(jnp.int32),
    }


ALPHA = 0.5
DATA_SCALE = 0.0625
SMOOTH = 4.0


def smoothing(blocks, neighbours):
    rows = blocks.astype(jnp.float32)
    near = jax.vmap(lambda block, index: jnp.take(block, index, axis=0))(rows, neighbours)
    return rows - jnp.sum(near, axis=2) / KNN


def reference(user_factors, item_factors, ratings, tile_cell, keep_count, send_count, user_nbrs, item_nbrs):
    user_tiles = user_factors.reshape(N_ROW, UT, TILE, RANK)
    counts = (keep_count + jnp.sum(send_count, axis=2)).astype(jnp.int32)

    def over_rows(item_acc, row_index):
        user_block = user_tiles[row_index]

        def over_cols(carry, col_index):
            user_acc, item_all = carry
            item_block = item_factors[col_index].reshape(VT, TILE, RANK)
            slot_ratings = ratings[row_index, col_index]
            slot_cells = tile_cell[row_index, col_index]

            def one_tile(slot, inner):
                user_part, item_part = inner
                cell = slot_cells[slot]
                upper = cell // VT
                lower = cell % VT
                left = user_block[upper]
                right = item_block[lower]
                product = jnp.dot(left, right.T, preferred_element_type=jnp.float32)
                values = slot_ratings[slot].astype(jnp.float32)
                prefer = jnp.where(values > 0, 1.0, 0.0).astype(jnp.float32)
                error = ((1.0 + ALPHA * values) * (product - prefer)).astype(jnp.bfloat16)
                user_part = user_part.at[upper].add(jnp.dot(error, right, preferred_element_type=jnp.float32))
                item_part = item_part.at[lower].add(jnp.dot(error.T, left, preferred_element_type=jnp.float32))
                return user_part, item_part

            item_col = item_all[col_index]
            user_acc, item_col = lax.fori_loop(0, counts[row_index, col_index], one_tile, (user_acc, item_col))
            item_all = item_all.at[col_index].set(item_col)
            return (user_acc, item_all), None

        start = (jnp.zeros((UT, TILE, RANK), jnp.float32), item_acc)
        (user_acc, item_acc), _ = lax.scan(over_cols, start, jnp.arange(N_COL))
        return item_acc, user_acc

    item_zero = jnp.zeros((N_COL, VT, TILE, RANK), jnp.float32)
    item_data, user_data = lax.scan(over_rows, item_zero, jnp.arange(N_ROW))
    user_smooth = smoothing(user_factors.reshape(N_ROW, UBLK, RANK), user_nbrs.reshape(N_ROW, UBLK, KNN))
    item_smooth = smoothing(item_factors, item_nbrs)
    grad_users = DATA_SCALE * user_data.reshape(USERS, RANK) + SMOOTH * user_smooth.reshape(USERS, RANK)
    grad_items = DATA_SCALE * item_data.reshape(N_COL, VBLK, RANK) + SMOOTH * item_smooth
    return grad_users, grad_items
```

```python
import functools

import jax
import jax.numpy as jnp
from jax import lax
from jax.experimental import pallas as pl
from jax.experimental.pallas import tpu as pltpu
from jax.sharding import PartitionSpec as P

ALPHA = 0.5
DATA_SCALE = 0.0625
SMOOTH = 4.0

NX, NY, NC = 4, 8, 2
CHIPS = NX * NY
MESH = pl.DeviceIdType.MESH
F32 = jnp.float32
BF16 = jnp.bfloat16


def ring_order(n):
    order = []
    for d in range(1, n // 2 + 1):
        order.append(d)
        if d != n - d:
            order.append(n - d)
    return order


def neighbour_counts(nbrs, width):
    nbrs = jnp.transpose(nbrs)
    rows, knn = nbrs.shape
    place = lax.broadcasted_iota(jnp.int32, (rows, width), 1)
    total = jnp.zeros((rows, width), F32)
    for k in range(knn):
        total = total + jnp.where(nbrs[:, k : k + 1] == place, 1.0, 0.0)
    return total.astype(BF16)


def kernel(
    nrow, lag,
    uf, vf, ratings, cells, keep, sends, unbr, vnbr,
    gu, gi,
    ug, vg, rat, er, ua, it, itf, pr, us, ur, ist, ir, au, ai, invv, invs,
    y_recv, x_recv, p_recv, z_recv, pr_recv, ur_recv, ir_recv,
    y_send, x_send, p_send, z_send, pr_send, ur_send, ir_send, loc_sem, inv_sem,
):
    r = lax.axis_index("row")
    col = lax.axis_index("col")
    c = lax.rem(col, NC)
    other = 1 - c
    p = col // NC
    x = p // NY
    y = lax.rem(p, NY)
    slots, tile = ratings.shape[2], ratings.shape[3]
    vt = nrow * vf.shape[1] // tile
    steps = CHIPS // 4
    urows = uf.shape[0]
    irows = vf.shape[1]

    def dev(chip, core):
        return (r, chip * NC + core)

    def remote(src, dst, ssem, rsem, device):
        return pltpu.make_async_remote_copy(
            src_ref=src, dst_ref=dst, send_sem=ssem, recv_sem=rsem,
            device_id=device, device_id_type=MESH,
        )

    load = pltpu.make_async_copy(ratings.at[0, 0], rat, loc_sem)
    load.start()

    barrier = pltpu.get_barrier_semaphore()

    def greet_plane(d, _):
        chip = lax.rem(p + d, CHIPS)
        pl.semaphore_signal(barrier, inc=1, device_id=dev(chip, c), device_id_type=MESH)
        return 0

    def greet_z(d, _):
        pl.semaphore_signal(barrier, inc=1, device_id=(lax.rem(r + d, nrow), col), device_id_type=MESH)
        return 0

    lax.fori_loop(1, nrow, greet_z, 0)
    lax.fori_loop(1, CHIPS, greet_plane, 0)
    pl.semaphore_signal(barrier, inc=1, device_id=dev(p, other), device_id_type=MESH)

    live = keep[0, 0]
    for q in range(nrow):
        live = live + sends[0, 0, q]
    slot_at = lax.broadcasted_iota(jnp.int32, (128, slots), 1)
    cell_at = lax.broadcasted_iota(jnp.int32, (128, slots), 0)
    held = jnp.where((cells[0] == cell_at) & (slot_at < live), slot_at + 1, 0)
    by_cell = jnp.sum(held.astype(F32), axis=1, keepdims=True)
    wide = jnp.transpose(jnp.broadcast_to(by_cell, (128, 128)))
    invv[...] = wide[0:8, :].astype(jnp.int32)
    inv_copy = pltpu.make_async_copy(invv, invs, inv_sem)
    inv_copy.start()

    au[...] = neighbour_counts(unbr[...], au.shape[1])
    ai[...] = neighbour_counts(vnbr[0], ai.shape[1])
    ug[p, c] = uf[...]
    vg[r] = vf[0]
    ur[p] = jnp.zeros(ur.shape[1:], BF16)
    ir[r] = jnp.zeros(ir.shape[1:], BF16)
    it[...] = jnp.zeros_like(it)

    pl.semaphore_wait(barrier, nrow - 1 + CHIPS - 1 + 1)

    def send_z(d, _):
        to = lax.rem(r + d, nrow)
        remote(vf.at[0], vg.at[r], z_send, z_recv, (to, col)).start()
        return 0

    def send_y(d, _):
        chip = x * NY + lax.rem(y + d, NY)
        remote(uf, ug.at[p, c], y_send, y_recv.at[y], dev(chip, c)).start()
        return 0

    def spread_x(src, chip):
        def one(d, _):
            to = lax.rem(x + d, NX) * NY + y
            remote(src, ug.at[chip, c], x_send, x_recv.at[chip], dev(to, c)).start()
            return 0

        lax.fori_loop(1, NX, one, 0)

    def to_partner(src, chip):
        remote(src, ug.at[chip, c], p_send, p_recv, dev(p, other)).start()

    lax.fori_loop(1, NY, send_y, 0)
    lax.fori_loop(1, nrow, send_z, 0)
    spread_x(uf, p)
    to_partner(uf, p)

    for d in ring_order(NY):
        yy = lax.rem(y + d, NY)
        chip = x * NY + yy
        piece = ug.at[chip, c]
        remote(piece, piece, y_send, y_recv.at[yy], dev(p, other)).wait_recv()
        spread_x(piece, chip)
        to_partner(piece, chip)
    for d in [0] + ring_order(NY):
        yy = lax.rem(y + d, NY)
        for dx in ring_order(NX):
            chip = lax.rem(x + dx, NX) * NY + yy
            piece = ug.at[chip, c]
            remote(piece, piece, x_send, x_recv.at[chip], dev(p, other)).wait_recv()
            to_partner(piece, chip)

    inv_copy.wait()
    load.wait()
    some = vg.at[pl.ds(0, nrow - 1)]
    remote(some, some, z_send, z_recv, dev(p, other)).wait_recv()
    some = ug.at[:, other]
    remote(some, some, p_send, p_recv, dev(p, other)).wait_recv()

    first = p // 4 + 1

    def pass_on(i):
        t = lax.rem(first + i + steps, steps)
        four = pl.ds(t * 4, 4)
        remote(pr.at[four], pr.at[four], pr_send, pr_recv.at[t], dev(p, other)).wait_recv()
        us[four] = (ua[four, c] + pr[four]).astype(BF16)

        def one(j, _):
            chip = t * 4 + j

            @pl.when(chip != p)
            def _():
                remote(us.at[chip], ur.at[p], ur_send, ur_recv, dev(chip, c)).start()

            return 0

        lax.fori_loop(0, 4, one, 0)

    def step(i, _):
        t = lax.rem(first + i, steps)
        four = pl.ds(t * 4, 4)
        users = ug[four].reshape(2 * tile, -1)
        for pair in range(vt // 2):
            items = vg[pl.ds(pair * (2 * tile // irows), 2 * tile // irows)].reshape(2 * tile, -1)
            product = lax.dot_general(
                users, items, (((1,), (1,)), ((), ())), preferred_element_type=F32
            )
            for a in range(2):
                for b in range(2):
                    slot = invs[0, (t * 2 + a) * vt + pair * 2 + b]
                    weight = jnp.minimum(slot, 1).astype(F32)
                    values = rat[jnp.clip(slot - 1, 0, slots - 1)].astype(F32)
                    prefer = jnp.where(values > 0, 1.0, 0.0).astype(F32)
                    part = product[a * tile : (a + 1) * tile, b * tile : (b + 1) * tile]
                    error = (weight + (ALPHA * weight) * values) * (part - prefer)
                    er[a * tile : (a + 1) * tile, (pair * 2 + b) * tile : (pair * 2 + b + 1) * tile] = error.astype(BF16)
        error = er[...]
        items = vg[...].reshape(vt * tile, -1)
        user_part = jnp.dot(error, items, preferred_element_type=F32)
        ua[four] = user_part.reshape(4, NC, urows, -1)
        it[...] += lax.dot_general(users, error, (((0,), (0,)), ((), ())), preferred_element_type=F32)
        remote(ua.at[four, other], pr.at[four], pr_send, pr_recv.at[t], dev(p, other)).start()

        @pl.when(i >= lag)
        def _():
            pass_on(i - lag)

        return 0

    lax.fori_loop(0, steps, step, 0)

    item_total = jnp.transpose(it[...]).reshape(nrow, irows, -1)
    itf[...] = item_total
    ist[...] = item_total.astype(BF16)

    def send_items(d, _):
        to = lax.rem(r + d, nrow)
        remote(ist.at[to], ir.at[r], ir_send, ir_recv, (to, col)).start()
        return 0

    lax.fori_loop(1, nrow, send_items, 0)
    for i in range(steps - lag, steps):
        pass_on(i)

    near = jnp.dot(au[...], ug[...].reshape(CHIPS * NC * urows, -1), preferred_element_type=F32)
    user_smooth = uf[...].astype(F32) - near / unbr.shape[0]
    near = jnp.dot(ai[...], vg[...].reshape(vt * tile, -1), preferred_element_type=F32)
    item_smooth = vf[0].astype(F32) - near / vnbr.shape[1]

    some = ur.at[pl.ds(0, CHIPS - 1)]
    remote(some, some, ur_send, ur_recv, dev(p, other)).wait_recv()
    total = ua[p, c] + pr[p] + jnp.sum(ur[...].astype(F32), axis=0)
    gu[...] = DATA_SCALE * total + SMOOTH * user_smooth
    some = ir.at[pl.ds(0, nrow - 1)]
    remote(some, some, ir_send, ir_recv, dev(p, other)).wait_recv()
    total = itf[r] + jnp.sum(ir[...].astype(F32), axis=0)
    gi[0] = DATA_SCALE * total + SMOOTH * item_smooth

    def left(view, sem):
        remote(view, view, sem, ur_recv, dev(p, other)).wait_send()

    left(ug.at[pl.ds(0, NY - 1), c], y_send)
    left(ug.at[pl.ds(0, (NX - 1) * NY), c], x_send)
    left(ug.at[:, c], p_send)
    left(vg.at[pl.ds(0, nrow - 1)], z_send)
    left(pr, pr_send)
    left(us.at[pl.ds(0, CHIPS - 1)], ur_send)
    left(ist.at[pl.ds(0, nrow - 1)], ir_send)


def finish(u_in, i_in, gu, gi):
    gu[...] = u_in[...]
    gi[...] = i_in[...]


def solution(mesh):
    nrow = mesh.shape["row"]
    placed = (
        P(("row", "col"), None),
        P("col", "row", None),
        P("row", "col", None, None, None),
        P("row", "col", None),
        P("row", "col"),
        P("row", "col", None),
        P(("row", "col"), None),
        P("col", "row", None),
    )

    def local(uf, vf, ratings, cells, keep, sends, unbr, vnbr):
        urows, rank = uf.shape
        irows = vf.shape[1]
        slots, tile = ratings.shape[2], ratings.shape[3]
        outs_shape = (
            jax.ShapeDtypeStruct((urows, rank), F32),
            jax.ShapeDtypeStruct((1, irows, rank), F32),
        )
        vmem = pl.BlockSpec(memory_space=pltpu.VMEM)
        smem = pl.BlockSpec(memory_space=pltpu.SMEM)
        hbm = pl.BlockSpec(memory_space=pl.ANY)
        dma = pltpu.SemaphoreType.DMA
        V = pltpu.VMEM
        outs = pl.pallas_call(
            functools.partial(kernel, nrow, 2),
            out_shape=outs_shape,
            in_specs=[vmem, vmem, hbm, vmem, smem, smem, vmem, vmem],
            out_specs=(vmem, vmem),
            scratch_shapes=[
                V((CHIPS, NC, urows, rank), BF16),
                V((nrow, irows, rank), BF16),
                V((slots, tile, tile), BF16),
                V((2 * tile, nrow * irows), BF16),
                V((CHIPS, NC, urows, rank), F32),
                V((rank, nrow * irows), F32),
                V((nrow, irows, rank), F32),
                V((CHIPS, urows, rank), F32),
                V((CHIPS, urows, rank), BF16),
                V((CHIPS, urows, rank), BF16),
                V((nrow, irows, rank), BF16),
                V((nrow, irows, rank), BF16),
                V((urows, CHIPS * NC * urows), BF16),
                V((irows, nrow * irows), BF16),
                V((8, 128), jnp.int32),
                pltpu.SMEM((8, 128), jnp.int32),
                dma((NY,)), dma((CHIPS,)), dma, dma, dma((CHIPS // 4,)), dma, dma,
                dma, dma, dma, dma, dma, dma, dma, dma, dma,
            ],
            compiler_params=pltpu.CompilerParams(collective_id=0, has_side_effects=True),
        )(uf, vf, ratings, cells, keep, sends, unbr.T, jnp.swapaxes(vnbr, 1, 2))
        return pl.pallas_call(
            finish,
            out_shape=outs_shape,
            in_specs=[vmem, vmem],
            out_specs=(vmem, vmem),
        )(*outs)

    return jax.shard_map(
        local,
        mesh=mesh,
        in_specs=placed,
        out_specs=(P(("row", "col"), None), P("col", "row", None)),
        check_vma=False,
    )
```

```python
import functools

import jax
import jax.numpy as jnp
from jax import lax
from jax.experimental import pallas as pl
from jax.experimental.pallas import tpu as pltpu
from jax.sharding import PartitionSpec as P

ALPHA = 0.5
DATA_SCALE = 0.0625
SMOOTH = 4.0

NX, NY, NC = 4, 8, 2
CHIPS = NX * NY
MESH = pl.DeviceIdType.MESH
F32 = jnp.float32
BF16 = jnp.bfloat16


def ring_order(n):
    order = []
    for d in range(1, n // 2 + 1):
        order.append(d)
        if d != n - d:
            order.append(n - d)
    return order


def far_first(n):
    return ring_order(n)[::-1]


def neighbour_counts(nbrs, width):
    nbrs = jnp.transpose(nbrs)
    rows, knn = nbrs.shape
    place = lax.broadcasted_iota(jnp.int32, (rows, width), 1)
    total = jnp.zeros((rows, width), F32)
    for k in range(knn):
        total = total + jnp.where(nbrs[:, k : k + 1] == place, 1.0, 0.0)
    return total.astype(BF16)


def kernel(
    nrow, lag,
    uf_hbm, vf_hbm, ratings, cells_hbm, keep_hbm, sends_hbm, unbr_hbm, vnbr_hbm,
    gu, gi,
    uf, vf, cells, keep, sends, unbr, vnbr,
    ug, vg, rat, er, ua, it, itf, pr, us, ur, ist, ir, au, ai, invv, invs,
    y_recv, x_recv, p_recv, z_recv, pr_recv, ur_recv, ir_recv,
    y_send, x_send, p_send, z_send, pr_send, ur_send, ir_send, loc_sem, inv_sem,
):
    r = lax.axis_index("row")
    col = lax.axis_index("col")
    c = lax.rem(col, NC)
    other = 1 - c
    p = col // NC
    x = p // NY
    y = lax.rem(p, NY)
    slots, tile = ratings.shape[2], ratings.shape[3]
    vt = nrow * vf.shape[1] // tile
    steps = CHIPS // 4
    urows = uf.shape[0]
    irows = vf.shape[1]

    def dev(chip, core):
        return (r, chip * NC + core)

    def remote(src, dst, ssem, rsem, device):
        return pltpu.make_async_remote_copy(
            src_ref=src, dst_ref=dst, send_sem=ssem, recv_sem=rsem,
            device_id=device, device_id_type=MESH,
        )

    loads = [
        pltpu.make_async_copy(src, dst, loc_sem.at[k])
        for k, (src, dst) in enumerate((
            (uf_hbm, uf), (vf_hbm, vf), (cells_hbm, cells), (keep_hbm, keep),
            (sends_hbm, sends), (unbr_hbm, unbr), (vnbr_hbm, vnbr), (ratings.at[0, 0], rat),
        ))
    ]

    barrier = pltpu.get_barrier_semaphore()

    def greet(device):
        pl.semaphore_signal(barrier, inc=1, device_id=device, device_id_type=MESH)

    def greet_y(d, _):
        greet(dev(x * NY + lax.rem(y + d, NY), c))
        return 0

    def greet_x(d, _):
        greet(dev(lax.rem(x + d, NX) * NY + y, c))
        return 0

    near_z = [3, nrow - 3, 2, nrow - 2, 1, nrow - 1]
    lax.fori_loop(1, NY, greet_y, 0)
    for d in near_z:
        greet((lax.rem(r + d, nrow), col))
    lax.fori_loop(1, NX, greet_x, 0)
    greet(dev(p, other))
    for copy in loads:
        copy.start()
    for copy in loads[:-1]:
        copy.wait()

    live = keep[...] + jnp.sum(sends[0], axis=1, keepdims=True)
    slot_at = lax.broadcasted_iota(jnp.int32, (128, slots), 1)
    cell_at = lax.broadcasted_iota(jnp.int32, (128, slots), 0)
    held = jnp.where((cells[0] == cell_at) & (slot_at < live), slot_at + 1, 0)
    by_cell = jnp.sum(held.astype(F32), axis=1, keepdims=True)
    wide = jnp.transpose(jnp.broadcast_to(by_cell, (128, 128)))
    invv[...] = wide[0:8, :].astype(jnp.int32)
    inv_copy = pltpu.make_async_copy(invv, invs, inv_sem)
    inv_copy.start()

    au[...] = neighbour_counts(unbr[...], au.shape[1])
    ai[...] = neighbour_counts(vnbr[0], ai.shape[1])
    ug[p, c] = uf[...]
    vg[r] = vf[0]
    ur[p] = jnp.zeros(ur.shape[1:], BF16)
    ir[r] = jnp.zeros(ir.shape[1:], BF16)
    it[...] = jnp.zeros_like(it)

    pl.semaphore_wait(barrier, NY - 1 + NX - 1 + len(near_z) + 1)

    def send_z(src, row, d):
        remote(src, vg.at[row], z_send, z_recv.at[row], (lax.rem(r + d, nrow), col)).start()

    def send_y(d):
        chip = x * NY + lax.rem(y + d, NY)
        remote(uf, ug.at[p, c], y_send, y_recv.at[y], dev(chip, c)).start()

    def spread_x(src, chip):
        def one(d, _):
            to = lax.rem(x + d, NX) * NY + y
            remote(src, ug.at[chip, c], x_send, x_recv.at[chip], dev(to, c)).start()
            return 0

        lax.fori_loop(1, NX, one, 0)

    def to_partner(src, chip):
        remote(src, ug.at[chip, c], p_send, p_recv, dev(p, other)).start()

    for d in far_first(NY):
        send_y(d)
    for d in near_z:
        send_z(vf.at[0], r, d)
    spread_x(uf, p)
    to_partner(uf, p)

    for d in ring_order(NY):
        yy = lax.rem(y + d, NY)
        chip = x * NY + yy
        piece = ug.at[chip, c]
        remote(piece, piece, y_send, y_recv.at[yy], dev(p, other)).wait_recv()
        spread_x(piece, chip)
        to_partner(piece, chip)
    for d in [nrow - 3, 1, nrow - 1, 2, nrow - 2, 3]:
        row = lax.rem(r + d, nrow)
        remote(vg.at[row], vg.at[row], z_send, z_recv.at[row], dev(p, other)).wait_recv()
        if d > nrow // 2:
            send_z(vg.at[row], row, 3)
        elif d < 3:
            send_z(vg.at[row], row, nrow - 3)
    for d in [0] + ring_order(NY):
        yy = lax.rem(y + d, NY)
        for dx in ring_order(NX):
            chip = lax.rem(x + dx, NX) * NY + yy
            piece = ug.at[chip, c]
            remote(piece, piece, x_send, x_recv.at[chip], dev(p, other)).wait_recv()
            to_partner(piece, chip)

    inv_copy.wait()
    loads[-1].wait()
    for d in range(4, nrow - 3):
        row = lax.rem(r + d, nrow)
        remote(vg.at[row], vg.at[row], z_send, z_recv.at[row], dev(p, other)).wait_recv()
    some = ug.at[:, other]
    remote(some, some, p_send, p_recv, dev(p, other)).wait_recv()

    first = p // 4 + 1

    def pass_on(i):
        t = lax.rem(first + i + steps, steps)
        four = pl.ds(t * 4, 4)
        remote(pr.at[four], pr.at[four], pr_send, pr_recv.at[t], dev(p, other)).wait_recv()
        us[four] = (ua[four, c] + pr[four]).astype(BF16)

        def one(j, _):
            chip = t * 4 + j

            @pl.when(chip != p)
            def _():
                remote(us.at[chip], ur.at[p], ur_send, ur_recv, dev(chip, c)).start()

            return 0

        lax.fori_loop(0, 4, one, 0)

    def step(i, _):
        t = lax.rem(first + i, steps)
        four = pl.ds(t * 4, 4)
        users = ug[four].reshape(2 * tile, -1)
        for pair in range(vt // 2):
            items = vg[pl.ds(pair * (2 * tile // irows), 2 * tile // irows)].reshape(2 * tile, -1)
            product = lax.dot_general(
                users, items, (((1,), (1,)), ((), ())), preferred_element_type=F32
            )
            for a in range(2):
                for b in range(2):
                    slot = invs[0, (t * 2 + a) * vt + pair * 2 + b]
                    weight = jnp.minimum(slot, 1).astype(F32)
                    values = rat[jnp.clip(slot - 1, 0, slots - 1)].astype(F32)
                    prefer = jnp.where(values > 0, 1.0, 0.0).astype(F32)
                    part = product[a * tile : (a + 1) * tile, b * tile : (b + 1) * tile]
                    error = (weight + (ALPHA * weight) * values) * (part - prefer)
                    er[a * tile : (a + 1) * tile, (pair * 2 + b) * tile : (pair * 2 + b + 1) * tile] = error.astype(BF16)
        error = er[...]
        items = vg[...].reshape(vt * tile, -1)
        user_part = jnp.dot(error, items, preferred_element_type=F32)
        ua[four] = user_part.reshape(4, NC, urows, -1)
        it[...] += lax.dot_general(users, error, (((0,), (0,)), ((), ())), preferred_element_type=F32)
        remote(ua.at[four, other], pr.at[four], pr_send, pr_recv.at[t], dev(p, other)).start()

        @pl.when(i >= lag)
        def _():
            pass_on(i - lag)

        return 0

    lax.fori_loop(0, steps, step, 0)

    item_total = jnp.transpose(it[...]).reshape(nrow, irows, -1)
    itf[...] = item_total
    ist[...] = item_total.astype(BF16)

    for d in far_first(nrow):
        to = lax.rem(r + d, nrow)
        remote(ist.at[to], ir.at[r], ir_send, ir_recv, (to, col)).start()
    for i in range(steps - lag, steps):
        pass_on(i)

    near = jnp.dot(au[...], ug[...].reshape(CHIPS * NC * urows, -1), preferred_element_type=F32)
    user_smooth = uf[...].astype(F32) - near / unbr.shape[0]
    near = jnp.dot(ai[...], vg[...].reshape(vt * tile, -1), preferred_element_type=F32)
    item_smooth = vf[0].astype(F32) - near / vnbr.shape[1]

    some = ur.at[pl.ds(0, CHIPS - 1)]
    remote(some, some, ur_send, ur_recv, dev(p, other)).wait_recv()
    total = ua[p, c] + pr[p] + jnp.sum(ur[...].astype(F32), axis=0)
    gu[...] = DATA_SCALE * total + SMOOTH * user_smooth
    some = ir.at[pl.ds(0, nrow - 1)]
    remote(some, some, ir_send, ir_recv, dev(p, other)).wait_recv()
    total = itf[r] + jnp.sum(ir[...].astype(F32), axis=0)
    gi[0] = DATA_SCALE * total + SMOOTH * item_smooth

    def left(view, sem):
        remote(view, view, sem, ur_recv, dev(p, other)).wait_send()

    left(ug.at[pl.ds(0, NY - 1), c], y_send)
    left(ug.at[pl.ds(0, (NX - 1) * NY), c], x_send)
    left(ug.at[:, c], p_send)
    left(vg.at[pl.ds(0, nrow - 1)], z_send)
    left(pr, pr_send)
    left(us.at[pl.ds(0, CHIPS - 1)], ur_send)
    left(ist.at[pl.ds(0, nrow - 1)], ir_send)


def finish(u_in, i_in, gu, gi):
    gu[...] = u_in[...]
    gi[...] = i_in[...]


def solution(mesh):
    nrow = mesh.shape["row"]
    placed = (
        P(("row", "col"), None),
        P("col", "row", None),
        P("row", "col", None, None, None),
        P("row", "col", None),
        P("row", "col"),
        P("row", "col", None),
        P(("row", "col"), None),
        P("col", "row", None),
    )

    def local(uf, vf, ratings, cells, keep, sends, unbr, vnbr):
        urows, rank = uf.shape
        irows = vf.shape[1]
        slots, tile = ratings.shape[2], ratings.shape[3]
        outs_shape = (
            jax.ShapeDtypeStruct((urows, rank), F32),
            jax.ShapeDtypeStruct((1, irows, rank), F32),
        )
        vmem = pl.BlockSpec(memory_space=pltpu.VMEM)
        hbm = pl.BlockSpec(memory_space=pltpu.HBM)
        dma = pltpu.SemaphoreType.DMA
        V = pltpu.VMEM
        outs = pl.pallas_call(
            functools.partial(kernel, nrow, 2),
            out_shape=outs_shape,
            in_specs=[hbm] * 8,
            out_specs=(vmem, vmem),
            scratch_shapes=[
                V((urows, rank), BF16),
                V((1, irows, rank), BF16),
                V(cells.shape, jnp.int32),
                V(keep.shape, jnp.int32),
                V(sends.shape, jnp.int32),
                V(unbr.shape[::-1], jnp.int32),
                V((1, vnbr.shape[2], irows), jnp.int32),
                V((CHIPS, NC, urows, rank), BF16),
                V((nrow, irows, rank), BF16),
                V((slots, tile, tile), BF16),
                V((2 * tile, nrow * irows), BF16),
                V((CHIPS, NC, urows, rank), F32),
                V((rank, nrow * irows), F32),
                V((nrow, irows, rank), F32),
                V((CHIPS, urows, rank), F32),
                V((CHIPS, urows, rank), BF16),
                V((CHIPS, urows, rank), BF16),
                V((nrow, irows, rank), BF16),
                V((nrow, irows, rank), BF16),
                V((urows, CHIPS * NC * urows), BF16),
                V((irows, nrow * irows), BF16),
                V((8, 128), jnp.int32),
                pltpu.SMEM((8, 128), jnp.int32),
                dma((NY,)), dma((CHIPS,)), dma, dma((nrow,)), dma((CHIPS // 4,)), dma, dma,
                dma, dma, dma, dma, dma, dma, dma, dma((8,)), dma,
            ],
            compiler_params=pltpu.CompilerParams(collective_id=0, has_side_effects=True),
        )(uf, vf, ratings, cells, keep, sends, unbr.T, jnp.swapaxes(vnbr, 1, 2))
        return pl.pallas_call(
            finish,
            out_shape=outs_shape,
            in_specs=[vmem, vmem],
            out_specs=(vmem, vmem),
        )(*outs)

    return jax.shard_map(
        local,
        mesh=mesh,
        in_specs=placed,
        out_specs=(P(("row", "col"), None), P("col", "row", None)),
        check_vma=False,
    )
```

```python
import functools

import jax
import jax.numpy as jnp
from jax import lax
from jax.experimental import pallas as pl
from jax.experimental.pallas import tpu as pltpu
from jax.sharding import PartitionSpec as P

ALPHA = 0.5
DATA_SCALE = 0.0625
SMOOTH = 4.0

NX, NY, NC = 4, 8, 2
CHIPS = NX * NY
MESH = pl.DeviceIdType.MESH
F32 = jnp.float32
BF16 = jnp.bfloat16


def ring_order(n):
    order = []
    for d in range(1, n // 2 + 1):
        order.append(d)
        if d != n - d:
            order.append(n - d)
    return order


def far_first(n):
    return ring_order(n)[::-1]


def neighbour_counts(nbrs, width):
    nbrs = jnp.transpose(nbrs)
    rows, knn = nbrs.shape
    place = lax.broadcasted_iota(jnp.int32, (rows, width), 1)
    total = jnp.zeros((rows, width), F32)
    for k in range(knn):
        total = total + jnp.where(nbrs[:, k : k + 1] == place, 1.0, 0.0)
    return total.astype(BF16)


def kernel(
    nrow, lag,
    uf_hbm, vf_hbm, ratings, cells_hbm, keep_hbm, sends_hbm, unbr_hbm, vnbr_hbm,
    gu, gi,
    uf, vf, cells, keep, sends, unbr, vnbr,
    ug, vg, rat, er, ua, it, itf, pr, us, ur, ist, ir, au, ai, invv, invs,
    y_recv, x_recv, p_recv, z_recv, pr_recv, ur_recv, ir_recv,
    y_send, x_send, p_send, z_send, pr_send, ur_send, ir_send, loc_sem, inv_sem,
):
    r = lax.axis_index("row")
    col = lax.axis_index("col")
    c = lax.rem(col, NC)
    other = 1 - c
    p = col // NC
    x = p // NY
    y = lax.rem(p, NY)
    slots, tile = ratings.shape[2], ratings.shape[3]
    vt = nrow * vf.shape[1] // tile
    steps = CHIPS // 4
    urows = uf.shape[0]
    irows = vf.shape[1]

    def dev(chip, core):
        return (r, chip * NC + core)

    def remote(src, dst, ssem, rsem, device):
        return pltpu.make_async_remote_copy(
            src_ref=src, dst_ref=dst, send_sem=ssem, recv_sem=rsem,
            device_id=device, device_id_type=MESH,
        )

    loads = [
        pltpu.make_async_copy(src, dst, loc_sem.at[k])
        for k, (src, dst) in enumerate((
            (uf_hbm, uf), (vf_hbm, vf), (cells_hbm, cells), (keep_hbm, keep),
            (sends_hbm, sends), (unbr_hbm, unbr), (vnbr_hbm, vnbr), (ratings.at[0, 0], rat),
        ))
    ]

    barrier = pltpu.get_barrier_semaphore()

    def greet(device):
        pl.semaphore_signal(barrier, inc=1, device_id=device, device_id_type=MESH)

    def greet_y(d, _):
        greet(dev(x * NY + lax.rem(y + d, NY), c))
        return 0

    def greet_x(d, _):
        greet(dev(lax.rem(x + d, NX) * NY + y, c))
        return 0

    near_z = [3, nrow - 3, 2, nrow - 2, 1, nrow - 1]
    lax.fori_loop(1, NY, greet_y, 0)
    for d in near_z:
        greet((lax.rem(r + d, nrow), col))
    lax.fori_loop(1, NX, greet_x, 0)
    greet(dev(p, other))
    for copy in loads:
        copy.start()
    for copy in loads[:-1]:
        copy.wait()

    live = keep[...] + jnp.sum(sends[0], axis=1, keepdims=True)
    slot_at = lax.broadcasted_iota(jnp.int32, (128, slots), 1)
    cell_at = lax.broadcasted_iota(jnp.int32, (128, slots), 0)
    held = jnp.where((cells[0] == cell_at) & (slot_at < live), slot_at + 1, 0)
    by_cell = jnp.sum(held.astype(F32), axis=1, keepdims=True)
    wide = jnp.transpose(jnp.broadcast_to(by_cell, (128, 128)))
    invv[...] = wide[0:8, :].astype(jnp.int32)
    inv_copy = pltpu.make_async_copy(invv, invs, inv_sem)
    inv_copy.start()

    ug[p, c] = uf[...]
    vg[r] = vf[0]
    ur[p] = jnp.zeros(ur.shape[1:], BF16)
    ir[r] = jnp.zeros(ir.shape[1:], BF16)

    pl.semaphore_wait(barrier, NY - 1 + NX - 1 + len(near_z) + 1)

    def send_z(src, row, d):
        remote(src, vg.at[row], z_send, z_recv.at[row], (lax.rem(r + d, nrow), col)).start()

    def send_y(d):
        chip = x * NY + lax.rem(y + d, NY)
        remote(uf, ug.at[p, c], y_send, y_recv.at[y], dev(chip, c)).start()

    def spread_x(src, chip):
        def one(d, _):
            to = lax.rem(x + d, NX) * NY + y
            remote(src, ug.at[chip, c], x_send, x_recv.at[chip], dev(to, c)).start()
            return 0

        lax.fori_loop(1, NX, one, 0)

    def to_partner(src, chip):
        remote(src, ug.at[chip, c], p_send, p_recv, dev(p, other)).start()

    for d in far_first(NY):
        send_y(d)
    for d in near_z:
        send_z(vf.at[0], r, d)
    spread_x(uf, p)
    to_partner(uf, p)

    for d in ring_order(NY):
        yy = lax.rem(y + d, NY)
        chip = x * NY + yy
        piece = ug.at[chip, c]
        remote(piece, piece, y_send, y_recv.at[yy], dev(p, other)).wait_recv()
        spread_x(piece, chip)
        to_partner(piece, chip)
    for d in [nrow - 3, 1, nrow - 1, 2, nrow - 2, 3]:
        row = lax.rem(r + d, nrow)
        remote(vg.at[row], vg.at[row], z_send, z_recv.at[row], dev(p, other)).wait_recv()
        if d > nrow // 2:
            send_z(vg.at[row], row, 3)
        elif d < 3:
            send_z(vg.at[row], row, nrow - 3)
    for d in [0] + ring_order(NY):
        yy = lax.rem(y + d, NY)
        for dx in ring_order(NX):
            chip = lax.rem(x + dx, NX) * NY + yy
            piece = ug.at[chip, c]
            remote(piece, piece, x_send, x_recv.at[chip], dev(p, other)).wait_recv()
            to_partner(piece, chip)

    inv_copy.wait()
    loads[-1].wait()
    for d in range(4, nrow - 3):
        row = lax.rem(r + d, nrow)
        remote(vg.at[row], vg.at[row], z_send, z_recv.at[row], dev(p, other)).wait_recv()
    some = ug.at[:, other]
    remote(some, some, p_send, p_recv, dev(p, other)).wait_recv()

    first = p // 4 + 1

    def group(i):
        return lax.rem(first + i, steps)

    def pass_on(i):
        remote(pr.at[i], pr.at[i], pr_send, pr_recv.at[i], dev(p, other)).wait_recv()
        us[i] = (ua[i, :, c] + pr[i]).astype(BF16)

        def one(j, _):
            chip = group(i) * 4 + j

            @pl.when(chip != p)
            def _():
                remote(us.at[i, j], ur.at[p], ur_send, ur_recv, dev(chip, c)).start()

            return 0

        lax.fori_loop(0, 4, one, 0)

    span = 2 * tile // irows
    own_pair = r // span
    pairs = vt // 2
    for turn in range(pairs):
        last = turn == pairs - 1
        pair = own_pair if last else lax.rem(own_pair + 1 + turn, pairs)
        rows = pl.ds(pair * span, span)
        items = vg[rows].reshape(2 * tile, -1)

        def produce(j):
            for i in (2 * j, 2 * j + 1):
                t = group(i)
                users = ug[pl.ds(t * 4, 4)].reshape(2 * tile, -1)
                product = lax.dot_general(
                    users, items, (((1,), (1,)), ((), ())), preferred_element_type=F32
                )
                for a in range(2):
                    for b in range(2):
                        slot = invs[0, (t * 2 + a) * vt + pair * 2 + b]
                        weight = jnp.minimum(slot, 1).astype(F32)
                        values = rat[jnp.clip(slot - 1, 0, slots - 1)].astype(F32)
                        prefer = jnp.where(values > 0, 1.0, 0.0).astype(F32)
                        part = product[a * tile : (a + 1) * tile, b * tile : (b + 1) * tile]
                        error = (weight + (ALPHA * weight) * values) * (part - prefer)
                        er[i, a * tile : (a + 1) * tile, b * tile : (b + 1) * tile] = error.astype(BF16)

        def consume(j):
            two = slice(2 * j, 2 * j + 2)
            error = er[two].reshape(4 * tile, -1)
            user_part = jnp.dot(error, items, preferred_element_type=F32)
            user_part = user_part.reshape(2, 4, NC, urows, -1)
            ua[two] = user_part if turn == 0 else ua[two] + user_part
            users = jnp.concatenate(
                [ug[pl.ds(group(i) * 4, 4)].reshape(2 * tile, -1) for i in (2 * j, 2 * j + 1)], axis=0
            )
            item_part = lax.dot_general(
                users, error, (((0,), (0,)), ((), ())), preferred_element_type=F32
            )
            it[...] = item_part if j == 0 else it[...] + item_part

        produce(0)
        for j in range(steps // 2):
            if j + 1 < steps // 2:
                produce(j + 1)
            consume(j)
            if last:
                for i in (2 * j, 2 * j + 1):
                    remote(ua.at[i, :, other], pr.at[i], pr_send, pr_recv.at[i], dev(p, other)).start()
                if j >= lag:
                    pass_on(2 * (j - lag))
                    pass_on(2 * (j - lag) + 1)

        done = jnp.transpose(it[...]).reshape(span, irows, -1)
        itf[rows] = done
        ist[rows] = done.astype(BF16)

        def send_item(j, _, pair=pair):
            to = pair * span + j

            @pl.when(to != r)
            def _():
                remote(ist.at[to], ir.at[r], ir_send, ir_recv, (to, col)).start()

            return 0

        lax.fori_loop(0, span, send_item, 0)
    for i in range(steps - 2 * lag, steps):
        pass_on(i)

    au[...] = neighbour_counts(unbr[...], au.shape[1])
    ai[...] = neighbour_counts(vnbr[0], ai.shape[1])
    near = jnp.dot(au[...], ug[...].reshape(CHIPS * NC * urows, -1), preferred_element_type=F32)
    user_smooth = uf[...].astype(F32) - near / unbr.shape[0]
    near = jnp.dot(ai[...], vg[...].reshape(vt * tile, -1), preferred_element_type=F32)
    item_smooth = vf[0].astype(F32) - near / vnbr.shape[1]

    some = ur.at[pl.ds(0, CHIPS - 1)]
    remote(some, some, ur_send, ur_recv, dev(p, other)).wait_recv()
    mine = lax.rem(p, 4)
    total = ua[steps - 1, mine, c] + pr[steps - 1, mine] + jnp.sum(ur[...].astype(F32), axis=0)
    gu[...] = DATA_SCALE * total + SMOOTH * user_smooth
    some = ir.at[pl.ds(0, nrow - 1)]
    remote(some, some, ir_send, ir_recv, dev(p, other)).wait_recv()
    total = itf[r] + jnp.sum(ir[...].astype(F32), axis=0)
    gi[0] = DATA_SCALE * total + SMOOTH * item_smooth

    def left(view, sem):
        remote(view, view, sem, ur_recv, dev(p, other)).wait_send()

    left(ug.at[pl.ds(0, NY - 1), c], y_send)
    left(ug.at[pl.ds(0, (NX - 1) * NY), c], x_send)
    left(ug.at[:, c], p_send)
    left(vg.at[pl.ds(0, nrow - 1)], z_send)
    left(pr, pr_send)
    left(ur.at[pl.ds(0, CHIPS - 1)], ur_send)
    left(ist.at[pl.ds(0, nrow - 1)], ir_send)


def finish(u_in, i_in, gu, gi):
    gu[...] = u_in[...]
    gi[...] = i_in[...]


def solution(mesh):
    nrow = mesh.shape["row"]
    placed = (
        P(("row", "col"), None),
        P("col", "row", None),
        P("row", "col", None, None, None),
        P("row", "col", None),
        P("row", "col"),
        P("row", "col", None),
        P(("row", "col"), None),
        P("col", "row", None),
    )

    def local(uf, vf, ratings, cells, keep, sends, unbr, vnbr):
        urows, rank = uf.shape
        irows = vf.shape[1]
        slots, tile = ratings.shape[2], ratings.shape[3]
        outs_shape = (
            jax.ShapeDtypeStruct((urows, rank), F32),
            jax.ShapeDtypeStruct((1, irows, rank), F32),
        )
        vmem = pl.BlockSpec(memory_space=pltpu.VMEM)
        hbm = pl.BlockSpec(memory_space=pltpu.HBM)
        dma = pltpu.SemaphoreType.DMA
        V = pltpu.VMEM
        outs = pl.pallas_call(
            functools.partial(kernel, nrow, 1),
            out_shape=(V((urows, rank), F32), V((1, irows, rank), F32)),
            in_specs=[hbm] * 8,
            out_specs=(vmem, vmem),
            scratch_shapes=[
                V((urows, rank), BF16),
                V((1, irows, rank), BF16),
                V(cells.shape, jnp.int32),
                V(keep.shape, jnp.int32),
                V(sends.shape, jnp.int32),
                V(unbr.shape[::-1], jnp.int32),
                V((1, vnbr.shape[2], irows), jnp.int32),
                V((CHIPS, NC, urows, rank), BF16),
                V((nrow, irows, rank), BF16),
                V((slots, tile, tile), BF16),
                V((CHIPS // 4, 2 * tile, 2 * tile), BF16),
                V((CHIPS // 4, 4, NC, urows, rank), F32),
                V((rank, 2 * tile), F32),
                V((nrow, irows, rank), F32),
                V((CHIPS // 4, 4, urows, rank), F32),
                V((CHIPS // 4, 4, urows, rank), BF16),
                V((CHIPS, urows, rank), BF16),
                V((nrow, irows, rank), BF16),
                V((nrow, irows, rank), BF16),
                V((urows, CHIPS * NC * urows), BF16),
                V((irows, nrow * irows), BF16),
                V((8, 128), jnp.int32),
                pltpu.SMEM((8, 128), jnp.int32),
                dma((NY,)), dma((CHIPS,)), dma, dma((nrow,)), dma((CHIPS // 4,)), dma, dma,
                dma, dma, dma, dma, dma, dma, dma, dma((8,)), dma,
            ],
            compiler_params=pltpu.CompilerParams(collective_id=0, has_side_effects=True),
        )(uf, vf, ratings, cells, keep, sends, unbr.T, jnp.swapaxes(vnbr, 1, 2))
        return pl.pallas_call(
            finish,
            out_shape=outs_shape,
            in_specs=[vmem, vmem],
            out_specs=(vmem, vmem),
        )(*(pltpu.with_memory_space_constraint(o, pltpu.VMEM) for o in outs))

    return jax.shard_map(
        local,
        mesh=mesh,
        in_specs=placed,
        out_specs=(P(("row", "col"), None), P("col", "row", None)),
        check_vma=False,
    )
```

```python
import functools

import jax
import jax.numpy as jnp
from jax import lax
from jax.experimental import pallas as pl
from jax.experimental.pallas import tpu as pltpu
from jax.sharding import PartitionSpec as P

ALPHA = 0.5
DATA_SCALE = 0.0625
SMOOTH = 4.0

NX, NY, NC = 4, 8, 2
CHIPS = NX * NY
MESH = pl.DeviceIdType.MESH
F32 = jnp.float32
BF16 = jnp.bfloat16


def ring_order(n):
    order = []
    for d in range(1, n // 2 + 1):
        order.append(d)
        if d != n - d:
            order.append(n - d)
    return order


def far_first(n):
    return ring_order(n)[::-1]


def neighbour_counts(nbrs, width):
    nbrs = jnp.transpose(nbrs)
    rows, knn = nbrs.shape
    place = lax.broadcasted_iota(jnp.int32, (rows, width), 1)
    total = jnp.zeros((rows, width), F32)
    for k in range(knn):
        total = total + jnp.where(nbrs[:, k : k + 1] == place, 1.0, 0.0)
    return total.astype(BF16)


def kernel(
    nrow, lag,
    uf_hbm, vf_hbm, ratings, cells_hbm, keep_hbm, sends_hbm, unbr_hbm, vnbr_hbm,
    gu, gi,
    uf, vf, cells, keep, sends, unbr, vnbr,
    ug, vg, rat, er, ua, it, itf, pr, us, ur, ist, ir, au, ai, invv, invs,
    y_recv, x_recv, p_recv, z_recv, pr_recv, ur_recv, ir_recv,
    y_send, x_send, p_send, z_send, pr_send, ur_send, ir_send, loc_sem, inv_sem,
):
    r = lax.axis_index("row")
    col = lax.axis_index("col")
    c = lax.rem(col, NC)
    other = 1 - c
    p = col // NC
    x = p // NY
    y = lax.rem(p, NY)
    slots, tile = ratings.shape[2], ratings.shape[3]
    vt = nrow * vf.shape[1] // tile
    steps = CHIPS // 4
    urows = uf.shape[0]
    irows = vf.shape[1]

    def dev(chip, core):
        return (r, chip * NC + core)

    def remote(src, dst, ssem, rsem, device):
        return pltpu.make_async_remote_copy(
            src_ref=src, dst_ref=dst, send_sem=ssem, recv_sem=rsem,
            device_id=device, device_id_type=MESH,
        )

    loads = [
        pltpu.make_async_copy(src, dst, loc_sem.at[k])
        for k, (src, dst) in enumerate((
            (uf_hbm, uf), (vf_hbm, vf), (cells_hbm, cells), (keep_hbm, keep),
            (sends_hbm, sends), (unbr_hbm, unbr), (vnbr_hbm, vnbr), (ratings.at[0, 0], rat),
        ))
    ]

    barrier = pltpu.get_barrier_semaphore()

    def greet(device):
        pl.semaphore_signal(barrier, inc=1, device_id=device, device_id_type=MESH)

    def greet_y(d, _):
        greet(dev(x * NY + lax.rem(y + d, NY), c))
        return 0

    def greet_x(d, _):
        greet(dev(lax.rem(x + d, NX) * NY + y, c))
        return 0

    near_z = [3, nrow - 3, 2, nrow - 2, 1, nrow - 1]
    lax.fori_loop(1, NY, greet_y, 0)
    for d in near_z:
        greet((lax.rem(r + d, nrow), col))
    lax.fori_loop(1, NX, greet_x, 0)
    greet(dev(p, other))
    for copy in loads:
        copy.start()
    for copy in loads[:-1]:
        copy.wait()

    live = keep[...] + jnp.sum(sends[0], axis=1, keepdims=True)
    slot_at = lax.broadcasted_iota(jnp.int32, (128, slots), 1)
    cell_at = lax.broadcasted_iota(jnp.int32, (128, slots), 0)
    held = jnp.where((cells[0] == cell_at) & (slot_at < live), slot_at + 1, 0)
    by_cell = jnp.sum(held.astype(F32), axis=1, keepdims=True)
    wide = jnp.transpose(jnp.broadcast_to(by_cell, (128, 128)))
    invv[...] = wide[0:8, :].astype(jnp.int32)
    inv_copy = pltpu.make_async_copy(invv, invs, inv_sem)
    inv_copy.start()

    ug[p, c] = uf[...]
    vg[r] = vf[0]
    ur[p] = jnp.zeros(ur.shape[1:], BF16)
    ir[r] = jnp.zeros(ir.shape[1:], BF16)

    pl.semaphore_wait(barrier, NY - 1 + NX - 1 + len(near_z) + 1)

    def send_z(src, row, d):
        remote(src, vg.at[row], z_send, z_recv.at[row], (lax.rem(r + d, nrow), col)).start()

    def send_y(d):
        chip = x * NY + lax.rem(y + d, NY)
        remote(uf, ug.at[p, c], y_send, y_recv.at[y], dev(chip, c)).start()

    def spread_x(src, chip):
        def one(d, _):
            to = lax.rem(x + d, NX) * NY + y
            remote(src, ug.at[chip, c], x_send, x_recv.at[chip], dev(to, c)).start()
            return 0

        lax.fori_loop(1, NX, one, 0)

    def to_partner(src, chip):
        remote(src, ug.at[chip, c], p_send, p_recv, dev(p, other)).start()

    for d in far_first(NY):
        send_y(d)
    for d in near_z:
        send_z(vf.at[0], r, d)
    spread_x(uf, p)
    to_partner(uf, p)

    for d in ring_order(NY):
        yy = lax.rem(y + d, NY)
        chip = x * NY + yy
        piece = ug.at[chip, c]
        remote(piece, piece, y_send, y_recv.at[yy], dev(p, other)).wait_recv()
        spread_x(piece, chip)
        to_partner(piece, chip)
    for d in [nrow - 3, 1, nrow - 1, 2, nrow - 2, 3]:
        row = lax.rem(r + d, nrow)
        remote(vg.at[row], vg.at[row], z_send, z_recv.at[row], dev(p, other)).wait_recv()
        if d > nrow // 2:
            send_z(vg.at[row], row, 3)
        elif d < 3:
            send_z(vg.at[row], row, nrow - 3)
    for d in [0] + ring_order(NY):
        yy = lax.rem(y + d, NY)
        for dx in ring_order(NX):
            chip = lax.rem(x + dx, NX) * NY + yy
            piece = ug.at[chip, c]
            remote(piece, piece, x_send, x_recv.at[chip], dev(p, other)).wait_recv()
            to_partner(piece, chip)

    inv_copy.wait()
    loads[-1].wait()
    for d in range(4, nrow - 3):
        row = lax.rem(r + d, nrow)
        remote(vg.at[row], vg.at[row], z_send, z_recv.at[row], dev(p, other)).wait_recv()
    some = ug.at[:, other]
    remote(some, some, p_send, p_recv, dev(p, other)).wait_recv()

    first = p // 4 + 1

    def group(i):
        return lax.rem(first + i, steps)

    def pass_on(i):
        remote(pr.at[i], pr.at[i], pr_send, pr_recv.at[i], dev(p, other)).wait_recv()
        us[i] = (ua[i, :, c] + pr[i]).astype(BF16)

        def one(j, _):
            chip = group(i) * 4 + j

            @pl.when(chip != p)
            def _():
                remote(us.at[i, j], ur.at[p], ur_send, ur_recv, dev(chip, c)).start()

            return 0

        lax.fori_loop(0, 4, one, 0)

    span = 2 * tile // irows
    own_pair = r // span
    pairs = vt // 2
    for turn in range(2):
        last = turn == 1
        held = [own_pair] if last else [lax.rem(own_pair + k, pairs) for k in range(1, pairs)]
        width = 2 * tile * len(held)
        items = jnp.concatenate([vg[pl.ds(pair * span, span)].reshape(2 * tile, -1) for pair in held], axis=0)

        def produce(j):
            for i in (2 * j, 2 * j + 1):
                t = group(i)
                users = ug[pl.ds(t * 4, 4)].reshape(2 * tile, -1)
                product = lax.dot_general(
                    users, items, (((1,), (1,)), ((), ())), preferred_element_type=F32
                )
                for a in range(2):
                    for b in range(2 * len(held)):
                        slot = invs[0, (t * 2 + a) * vt + held[b // 2] * 2 + b % 2]
                        weight = jnp.minimum(slot, 1).astype(F32)
                        values = rat[jnp.clip(slot - 1, 0, slots - 1)].astype(F32)
                        prefer = jnp.where(values > 0, 1.0, 0.0).astype(F32)
                        part = product[a * tile : (a + 1) * tile, b * tile : (b + 1) * tile]
                        error = (weight + (ALPHA * weight) * values) * (part - prefer)
                        er[i, a * tile : (a + 1) * tile, b * tile : (b + 1) * tile] = error.astype(BF16)

        def consume(j):
            two = slice(2 * j, 2 * j + 2)
            error = er[two, :, :width].reshape(4 * tile, width)
            user_part = jnp.dot(error, items, preferred_element_type=F32)
            user_part = user_part.reshape(2, 4, NC, urows, -1)
            ua[two] = user_part if turn == 0 else ua[two] + user_part
            users = jnp.concatenate(
                [ug[pl.ds(group(i) * 4, 4)].reshape(2 * tile, -1) for i in (2 * j, 2 * j + 1)], axis=0
            )
            item_part = lax.dot_general(
                users, error, (((0,), (0,)), ((), ())), preferred_element_type=F32
            )
            it[:, :width] = item_part if j == 0 else it[:, :width] + item_part

        produce(0)
        for j in range(steps // 2):
            if j + 1 < steps // 2:
                produce(j + 1)
            consume(j)
            if last:
                for i in (2 * j, 2 * j + 1):
                    remote(ua.at[i, :, other], pr.at[i], pr_send, pr_recv.at[i], dev(p, other)).start()
                if j >= lag:
                    pass_on(2 * (j - lag))
                    pass_on(2 * (j - lag) + 1)

        done = jnp.transpose(it[:, :width]).reshape(len(held), span, irows, -1)
        for k, pair in enumerate(held):
            itf[pl.ds(pair * span, span)] = done[k]
            ist[pl.ds(pair * span, span)] = done[k].astype(BF16)

        def send_item(j, pair):
            to = pair * span + j

            @pl.when(to != r)
            def _():
                remote(ist.at[to], ir.at[r], ir_send, ir_recv, (to, col)).start()

            return pair

        for pair in held:
            lax.fori_loop(0, span, send_item, pair)
    for i in range(steps - 2 * lag, steps):
        pass_on(i)

    au[...] = neighbour_counts(unbr[...], au.shape[1])
    ai[...] = neighbour_counts(vnbr[0], ai.shape[1])
    near = jnp.dot(au[...], ug[...].reshape(CHIPS * NC * urows, -1), preferred_element_type=F32)
    user_smooth = uf[...].astype(F32) - near / unbr.shape[0]
    near = jnp.dot(ai[...], vg[...].reshape(vt * tile, -1), preferred_element_type=F32)
    item_smooth = vf[0].astype(F32) - near / vnbr.shape[1]

    some = ur.at[pl.ds(0, CHIPS - 1)]
    remote(some, some, ur_send, ur_recv, dev(p, other)).wait_recv()
    mine = lax.rem(p, 4)
    total = ua[steps - 1, mine, c] + pr[steps - 1, mine] + jnp.sum(ur[...].astype(F32), axis=0)
    gu[...] = DATA_SCALE * total + SMOOTH * user_smooth
    some = ir.at[pl.ds(0, nrow - 1)]
    remote(some, some, ir_send, ir_recv, dev(p, other)).wait_recv()
    total = itf[r] + jnp.sum(ir[...].astype(F32), axis=0)
    gi[0] = DATA_SCALE * total + SMOOTH * item_smooth

    def left(view, sem):
        remote(view, view, sem, ur_recv, dev(p, other)).wait_send()

    left(ug.at[pl.ds(0, NY - 1), c], y_send)
    left(ug.at[pl.ds(0, (NX - 1) * NY), c], x_send)
    left(ug.at[:, c], p_send)
    left(vg.at[pl.ds(0, nrow - 1)], z_send)
    left(pr, pr_send)
    left(ur.at[pl.ds(0, CHIPS - 1)], ur_send)
    left(ist.at[pl.ds(0, nrow - 1)], ir_send)


def finish(u_in, i_in, gu, gi):
    gu[...] = u_in[...]
    gi[...] = i_in[...]


def solution(mesh):
    nrow = mesh.shape["row"]
    placed = (
        P(("row", "col"), None),
        P("col", "row", None),
        P("row", "col", None, None, None),
        P("row", "col", None),
        P("row", "col"),
        P("row", "col", None),
        P(("row", "col"), None),
        P("col", "row", None),
    )

    def local(uf, vf, ratings, cells, keep, sends, unbr, vnbr):
        urows, rank = uf.shape
        irows = vf.shape[1]
        slots, tile = ratings.shape[2], ratings.shape[3]
        outs_shape = (
            jax.ShapeDtypeStruct((urows, rank), F32),
            jax.ShapeDtypeStruct((1, irows, rank), F32),
        )
        vmem = pl.BlockSpec(memory_space=pltpu.VMEM)
        hbm = pl.BlockSpec(memory_space=pltpu.HBM)
        dma = pltpu.SemaphoreType.DMA
        V = pltpu.VMEM
        outs = pl.pallas_call(
            functools.partial(kernel, nrow, 1),
            out_shape=(V((urows, rank), F32), V((1, irows, rank), F32)),
            in_specs=[hbm] * 8,
            out_specs=(vmem, vmem),
            scratch_shapes=[
                V((urows, rank), BF16),
                V((1, irows, rank), BF16),
                V(cells.shape, jnp.int32),
                V(keep.shape, jnp.int32),
                V(sends.shape, jnp.int32),
                V(unbr.shape[::-1], jnp.int32),
                V((1, vnbr.shape[2], irows), jnp.int32),
                V((CHIPS, NC, urows, rank), BF16),
                V((nrow, irows, rank), BF16),
                V((slots, tile, tile), BF16),
                V((CHIPS // 4, 2 * tile, nrow * irows - 2 * tile), BF16),
                V((CHIPS // 4, 4, NC, urows, rank), F32),
                V((rank, nrow * irows - 2 * tile), F32),
                V((nrow, irows, rank), F32),
                V((CHIPS // 4, 4, urows, rank), F32),
                V((CHIPS // 4, 4, urows, rank), BF16),
                V((CHIPS, urows, rank), BF16),
                V((nrow, irows, rank), BF16),
                V((nrow, irows, rank), BF16),
                V((urows, CHIPS * NC * urows), BF16),
                V((irows, nrow * irows), BF16),
                V((8, 128), jnp.int32),
                pltpu.SMEM((8, 128), jnp.int32),
                dma((NY,)), dma((CHIPS,)), dma, dma((nrow,)), dma((CHIPS // 4,)), dma, dma,
                dma, dma, dma, dma, dma, dma, dma, dma((8,)), dma,
            ],
            compiler_params=pltpu.CompilerParams(collective_id=0, has_side_effects=True),
        )(uf, vf, ratings, cells, keep, sends, unbr.T, jnp.swapaxes(vnbr, 1, 2))
        return pl.pallas_call(
            finish,
            out_shape=outs_shape,
            in_specs=[vmem, vmem],
            out_specs=(vmem, vmem),
        )(*(pltpu.with_memory_space_constraint(o, pltpu.VMEM) for o in outs))

    return jax.shard_map(
        local,
        mesh=mesh,
        in_specs=placed,
        out_specs=(P(("row", "col"), None), P("col", "row", None)),
        check_vma=False,
    )
```

```python
import functools

import jax
import jax.numpy as jnp
from jax import lax
from jax.experimental import pallas as pl
from jax.experimental.pallas import tpu as pltpu
from jax.sharding import PartitionSpec as P

ALPHA = 0.5
DATA_SCALE = 0.0625
SMOOTH = 4.0

NX, NY, NC = 4, 8, 2
CHIPS = NX * NY
MESH = pl.DeviceIdType.MESH
F32 = jnp.float32
BF16 = jnp.bfloat16


def ring_order(n):
    order = []
    for d in range(1, n // 2 + 1):
        order.append(d)
        if d != n - d:
            order.append(n - d)
    return order


def far_first(n):
    return ring_order(n)[::-1]


def neighbour_counts(nbrs, width):
    nbrs = jnp.transpose(nbrs)
    rows, knn = nbrs.shape
    place = lax.broadcasted_iota(jnp.int32, (rows, width), 1)
    total = jnp.zeros((rows, width), F32)
    for k in range(knn):
        total = total + jnp.where(nbrs[:, k : k + 1] == place, 1.0, 0.0)
    return total.astype(BF16)


def kernel(
    nrow, lag,
    uf_hbm, vf_hbm, ratings, cells_hbm, keep_hbm, sends_hbm, unbr_hbm, vnbr_hbm,
    gu, gi,
    uf, vf, cells, keep, sends, unbr, vnbr,
    ug, vg, rat, er, ua, it, itf, pr, us, ur, ist, ir, au, ai, invv, invs,
    y_recv, x_recv, p_recv, z_recv, pr_recv, ur_recv, ir_recv,
    y_send, x_send, p_send, z_send, pr_send, ur_send, ir_send, loc_sem, inv_sem,
):
    r = lax.axis_index("row")
    col = lax.axis_index("col")
    c = lax.rem(col, NC)
    other = 1 - c
    p = col // NC
    x = p // NY
    y = lax.rem(p, NY)
    slots, tile = ratings.shape[2], ratings.shape[3]
    vt = nrow * vf.shape[1] // tile
    steps = CHIPS // 4
    urows = uf.shape[0]
    irows = vf.shape[1]

    def dev(chip, core):
        return (r, chip * NC + core)

    def remote(src, dst, ssem, rsem, device):
        return pltpu.make_async_remote_copy(
            src_ref=src, dst_ref=dst, send_sem=ssem, recv_sem=rsem,
            device_id=device, device_id_type=MESH,
        )

    loads = [
        pltpu.make_async_copy(src, dst, loc_sem.at[k])
        for k, (src, dst) in enumerate((
            (uf_hbm, uf), (vf_hbm, vf), (cells_hbm, cells), (keep_hbm, keep),
            (sends_hbm, sends), (unbr_hbm, unbr), (vnbr_hbm, vnbr), (ratings.at[0, 0], rat),
        ))
    ]

    barrier = pltpu.get_barrier_semaphore()

    def greet(device):
        pl.semaphore_signal(barrier, inc=1, device_id=device, device_id_type=MESH)

    def greet_y(d, _):
        greet(dev(x * NY + lax.rem(y + d, NY), c))
        return 0

    def greet_x(d, _):
        greet(dev(lax.rem(x + d, NX) * NY + y, c))
        return 0

    near_z = [3, nrow - 3, 2, nrow - 2, 1, nrow - 1]
    lax.fori_loop(1, NY, greet_y, 0)
    for d in near_z:
        greet((lax.rem(r + d, nrow), col))
    lax.fori_loop(1, NX, greet_x, 0)
    greet(dev(p, other))
    for copy in loads:
        copy.start()
    for copy in loads[:-1]:
        copy.wait()

    live = keep[...] + jnp.sum(sends[0], axis=1, keepdims=True)
    slot_at = lax.broadcasted_iota(jnp.int32, (128, slots), 1)
    cell_at = lax.broadcasted_iota(jnp.int32, (128, slots), 0)
    held = jnp.where((cells[0] == cell_at) & (slot_at < live), slot_at + 1, 0)
    by_cell = jnp.sum(held.astype(F32), axis=1, keepdims=True)
    wide = jnp.transpose(jnp.broadcast_to(by_cell, (128, 128)))
    invv[...] = wide[0:8, :].astype(jnp.int32)
    inv_copy = pltpu.make_async_copy(invv, invs, inv_sem)
    inv_copy.start()

    ug[p, c] = uf[...]
    vg[r] = vf[0]
    ur[p] = jnp.zeros(ur.shape[1:], BF16)
    ir[r] = jnp.zeros(ir.shape[1:], BF16)

    pl.semaphore_wait(barrier, NY - 1 + NX - 1 + len(near_z) + 1)

    def send_z(src, row, d):
        remote(src, vg.at[row], z_send, z_recv.at[row], (lax.rem(r + d, nrow), col)).start()

    def send_y(d):
        chip = x * NY + lax.rem(y + d, NY)
        remote(uf, ug.at[p, c], y_send, y_recv.at[y], dev(chip, c)).start()

    def spread_x(src, chip):
        def one(d, _):
            to = lax.rem(x + d, NX) * NY + y
            remote(src, ug.at[chip, c], x_send, x_recv.at[chip], dev(to, c)).start()
            return 0

        lax.fori_loop(1, NX, one, 0)

    def to_partner(src, chip):
        remote(src, ug.at[chip, c], p_send, p_recv.at[chip // NY], dev(p, other)).start()

    for d in far_first(NY):
        send_y(d)
    for d in near_z:
        send_z(vf.at[0], r, d)
    spread_x(uf, p)
    to_partner(uf, p)

    for d in ring_order(NY):
        yy = lax.rem(y + d, NY)
        chip = x * NY + yy
        piece = ug.at[chip, c]
        remote(piece, piece, y_send, y_recv.at[yy], dev(p, other)).wait_recv()
        spread_x(piece, chip)
        to_partner(piece, chip)
    for d in [nrow - 3, 1, nrow - 1, 2, nrow - 2, 3]:
        row = lax.rem(r + d, nrow)
        remote(vg.at[row], vg.at[row], z_send, z_recv.at[row], dev(p, other)).wait_recv()
        if d > nrow // 2:
            send_z(vg.at[row], row, 3)
        elif d < 3:
            send_z(vg.at[row], row, nrow - 3)
    for d in [0] + ring_order(NY):
        yy = lax.rem(y + d, NY)
        for dx in ring_order(NX):
            chip = lax.rem(x + dx, NX) * NY + yy
            piece = ug.at[chip, c]
            remote(piece, piece, x_send, x_recv.at[chip], dev(p, other)).wait_recv()
            to_partner(piece, chip)

    inv_copy.wait()
    loads[-1].wait()

    def far_items():
        for d in range(4, nrow - 3):
            row = lax.rem(r + d, nrow)
            remote(vg.at[row], vg.at[row], z_send, z_recv.at[row], dev(p, other)).wait_recv()

    def partner_users(xx):
        some = ug.at[pl.ds(xx * NY, NY), other]
        remote(some, some, p_send, p_recv.at[xx], dev(p, other)).wait_recv()

    first = p // 4 + 1

    def group(i):
        return lax.rem(first + i, steps)

    def pass_on(i):
        remote(pr.at[i], pr.at[i], pr_send, pr_recv.at[i], dev(p, other)).wait_recv()
        us[i] = (ua[i, :, c] + pr[i]).astype(BF16)

        def one(j, _):
            chip = group(i) * 4 + j

            @pl.when(chip != p)
            def _():
                remote(us.at[i, j], ur.at[p], ur_send, ur_recv, dev(chip, c)).start()

            return 0

        lax.fori_loop(0, 4, one, 0)

    span = 2 * tile // irows
    own_pair = r // span
    pairs = vt // 2
    for turn in range(pairs):
        last = turn == pairs - 1
        pair = lax.rem(own_pair + 1 + turn, pairs)
        if turn == 0:
            far_items()
        rows = pl.ds(pair * span, span)
        items = vg[rows].reshape(2 * tile, -1)

        def visited(j, turn=turn):
            if turn:
                return group(2 * j), group(2 * j + 1)
            xx = lax.rem(x + ([0] + ring_order(NX))[j], NX)
            return 2 * xx, 2 * xx + 1

        def produce(j):
            for i, t in zip((2 * j, 2 * j + 1), visited(j)):
                users = ug[pl.ds(t * 4, 4)].reshape(2 * tile, -1)
                product = lax.dot_general(
                    users, items, (((1,), (1,)), ((), ())), preferred_element_type=F32
                )
                for a in range(2):
                    for b in range(2):
                        slot = invs[0, (t * 2 + a) * vt + pair * 2 + b]
                        weight = jnp.minimum(slot, 1).astype(F32)
                        values = rat[jnp.clip(slot - 1, 0, slots - 1)].astype(F32)
                        prefer = jnp.where(values > 0, 1.0, 0.0).astype(F32)
                        part = product[a * tile : (a + 1) * tile, b * tile : (b + 1) * tile]
                        error = (weight + (ALPHA * weight) * values) * (part - prefer)
                        er[i, a * tile : (a + 1) * tile, b * tile : (b + 1) * tile] = error.astype(BF16)

        def consume(j):
            two = slice(2 * j, 2 * j + 2)
            error = er[two].reshape(4 * tile, -1)
            user_part = jnp.dot(error, items, preferred_element_type=F32)
            user_part = user_part.reshape(2, 4, NC, urows, -1)
            if turn:
                ua[two] = ua[two] + user_part
            else:
                for k, t in enumerate(visited(j)):
                    ua[lax.rem(t - first + 2 * steps, steps)] = user_part[k]
            users = jnp.concatenate(
                [ug[pl.ds(t * 4, 4)].reshape(2 * tile, -1) for t in visited(j)], axis=0
            )
            item_part = lax.dot_general(
                users, error, (((0,), (0,)), ((), ())), preferred_element_type=F32
            )
            it[...] = item_part if j == 0 else it[...] + item_part

        for j in range(-1, steps // 2):
            if j + 1 < steps // 2:
                if turn == 0:
                    partner_users(visited(j + 1)[0] // 2)
                produce(j + 1)
            if j < 0:
                continue
            consume(j)
            if last:
                for i in (2 * j, 2 * j + 1):
                    remote(ua.at[i, :, other], pr.at[i], pr_send, pr_recv.at[i], dev(p, other)).start()
                if j >= lag:
                    pass_on(2 * (j - lag))
                    pass_on(2 * (j - lag) + 1)

        done = jnp.transpose(it[...]).reshape(span, irows, -1)
        itf[rows] = done
        ist[rows] = done.astype(BF16)

        def send_item(j, _, pair=pair):
            to = pair * span + j

            @pl.when(to != r)
            def _():
                remote(ist.at[to], ir.at[r], ir_send, ir_recv, (to, col)).start()

            return 0

        lax.fori_loop(0, span, send_item, 0)
    for i in range(steps - 2 * lag, steps):
        pass_on(i)

    au[...] = neighbour_counts(unbr[...], au.shape[1])
    ai[...] = neighbour_counts(vnbr[0], ai.shape[1])
    near = jnp.dot(au[...], ug[...].reshape(CHIPS * NC * urows, -1), preferred_element_type=F32)
    user_smooth = uf[...].astype(F32) - near / unbr.shape[0]
    near = jnp.dot(ai[...], vg[...].reshape(vt * tile, -1), preferred_element_type=F32)
    item_smooth = vf[0].astype(F32) - near / vnbr.shape[1]

    some = ur.at[pl.ds(0, CHIPS - 1)]
    remote(some, some, ur_send, ur_recv, dev(p, other)).wait_recv()
    mine = lax.rem(p, 4)
    total = ua[steps - 1, mine, c] + pr[steps - 1, mine] + jnp.sum(ur[...].astype(F32), axis=0)
    gu[...] = DATA_SCALE * total + SMOOTH * user_smooth
    some = ir.at[pl.ds(0, nrow - 1)]
    remote(some, some, ir_send, ir_recv, dev(p, other)).wait_recv()
    total = itf[r] + jnp.sum(ir[...].astype(F32), axis=0)
    gi[0] = DATA_SCALE * total + SMOOTH * item_smooth

    def left(view, sem):
        remote(view, view, sem, ur_recv, dev(p, other)).wait_send()

    left(ug.at[pl.ds(0, NY - 1), c], y_send)
    left(ug.at[pl.ds(0, (NX - 1) * NY), c], x_send)
    left(ug.at[:, c], p_send)
    left(vg.at[pl.ds(0, nrow - 1)], z_send)
    left(pr, pr_send)
    left(ur.at[pl.ds(0, CHIPS - 1)], ur_send)
    left(ist.at[pl.ds(0, nrow - 1)], ir_send)


def finish(u_in, i_in, gu, gi):
    gu[...] = u_in[...]
    gi[...] = i_in[...]


def solution(mesh):
    nrow = mesh.shape["row"]
    placed = (
        P(("row", "col"), None),
        P("col", "row", None),
        P("row", "col", None, None, None),
        P("row", "col", None),
        P("row", "col"),
        P("row", "col", None),
        P(("row", "col"), None),
        P("col", "row", None),
    )

    def local(uf, vf, ratings, cells, keep, sends, unbr, vnbr):
        urows, rank = uf.shape
        irows = vf.shape[1]
        slots, tile = ratings.shape[2], ratings.shape[3]
        outs_shape = (
            jax.ShapeDtypeStruct((urows, rank), F32),
            jax.ShapeDtypeStruct((1, irows, rank), F32),
        )
        vmem = pl.BlockSpec(memory_space=pltpu.VMEM)
        hbm = pl.BlockSpec(memory_space=pltpu.HBM)
        dma = pltpu.SemaphoreType.DMA
        V = pltpu.VMEM
        outs = pl.pallas_call(
            functools.partial(kernel, nrow, 1),
            out_shape=(V((urows, rank), F32), V((1, irows, rank), F32)),
            in_specs=[hbm] * 8,
            out_specs=(vmem, vmem),
            scratch_shapes=[
                V((urows, rank), BF16),
                V((1, irows, rank), BF16),
                V(cells.shape, jnp.int32),
                V(keep.shape, jnp.int32),
                V(sends.shape, jnp.int32),
                V(unbr.shape[::-1], jnp.int32),
                V((1, vnbr.shape[2], irows), jnp.int32),
                V((CHIPS, NC, urows, rank), BF16),
                V((nrow, irows, rank), BF16),
                V((slots, tile, tile), BF16),
                V((CHIPS // 4, 2 * tile, 2 * tile), BF16),
                V((CHIPS // 4, 4, NC, urows, rank), F32),
                V((rank, 2 * tile), F32),
                V((nrow, irows, rank), F32),
                V((CHIPS // 4, 4, urows, rank), F32),
                V((CHIPS // 4, 4, urows, rank), BF16),
                V((CHIPS, urows, rank), BF16),
                V((nrow, irows, rank), BF16),
                V((nrow, irows, rank), BF16),
                V((urows, CHIPS * NC * urows), BF16),
                V((irows, nrow * irows), BF16),
                V((8, 128), jnp.int32),
                pltpu.SMEM((8, 128), jnp.int32),
                dma((NY,)), dma((CHIPS,)), dma((NX,)), dma((nrow,)), dma((CHIPS // 4,)), dma, dma,
                dma, dma, dma, dma, dma, dma, dma, dma((8,)), dma,
            ],
            compiler_params=pltpu.CompilerParams(collective_id=0, has_side_effects=True),
        )(uf, vf, ratings, cells, keep, sends, unbr.T, jnp.swapaxes(vnbr, 1, 2))
        return pl.pallas_call(
            finish,
            out_shape=outs_shape,
            in_specs=[vmem, vmem],
            out_specs=(vmem, vmem),
        )(*(pltpu.with_memory_space_constraint(o, pltpu.VMEM) for o in outs))

    return jax.shard_map(
        local,
        mesh=mesh,
        in_specs=placed,
        out_specs=(P(("row", "col"), None), P("col", "row", None)),
        check_vma=False,
    )
```
